32 devices in a mesh: row: 8 (over z, core), col: 4 (over y, x).
Axes of the slice: x: 2, y: 2, z: 4, core: 2. Of those that a mesh axis runs over, the one named last changes fastest.
Arguments:
- example_sketch: float32 [512, 8192], P('col', 'row'), may hold values from -6 to 6
- candidate_sketch: float32 [512, 8192], P('row', 'col'), may hold values from -6 to 6
- best_start: float32 [8192], P('row'), may hold values from -1 to 1.5
- chosen: int32 [2], replicated, may hold values from 0 to 8191
Outputs:
- best: float32 [8192], P('row')
- gains: float32 [2, 8192], P(None, 'col')
The draws below stay inside these ranges and needn't reach their ends.
All inputs are finite; a program needn't handle non-finite values.
Results may differ from the reference program's by a relative error of at most 0.000075.
Values sent between devices are 32-bit elements; how exact they have to be, the bound alone decides.
No kernel may reach another device: no remote copies, remote signals or barrier semaphores. Data moves between devices by JAX's collectives and lax.ppermute only.
A program may use at most 64 MiB of HBM per device.

```python
import jax
import jax.numpy as jnp
from jax import lax

W = 512
C_DEV = 2048
ROUNDS = 2
EXAMPLES = 8192
CANDIDATES = 8192


def level_of(key, shape, cuts, least, largest):
    level = 1.0
    for axis_at, shards_of in cuts:
        draws = jax.random.uniform(jax.random.fold_in(jax.random.fold_in(key, 6), axis_at), (shards_of,), jnp.float32, least / len(cuts), largest / len(cuts))
        level = level * jnp.repeat(jnp.exp(draws), shape[axis_at] // shards_of).reshape((-1,) + (1,) * (len(shape) - 1 - axis_at))
    return level


def scatter_about(key, shape, scale, limit, shards=(), dtype=jnp.bfloat16):
    array = jax.random.normal(key, shape, jnp.float32) * scale
    if len(shards) > 0:
        array = level_of(key, shape, shards, -0.22, 0.18) * array
    return jnp.clip(array, min=-limit, max=limit).astype(dtype)


def setup_inputs(seed: int = 0) -> dict:
    key_list = jax.random.split(jax.random.key(seed), 5)
    example_sketch = scatter_about(key_list[0], (W, EXAMPLES), 1.0, 6.0, ((0, 4), (1, 8)), jnp.float32)
    candidate_sketch = scatter_about(key_list[1], (W, CANDIDATES), 1.0, 6.0, ((0, 8), (1, 4)), jnp.float32)
    best_start = jnp.clip(-1.0 + 2.5 * jax.random.uniform(key_list[2], (EXAMPLES,), jnp.float32) ** level_of(key_list[2], (EXAMPLES,), ((0, 8),), -0.2, 0.2), -1.0, 1.5)
    chosen = jax.random.randint(key_list[3], (ROUNDS,), 0, CANDIDATES).astype(jnp.int32)
    return dict(example_sketch=example_sketch, candidate_sketch=candidate_sketch, best_start=best_start, chosen=chosen)


EPS = 1e-06

def reference(example_sketch, candidate_sketch, best_start, chosen):
    scale = jnp.sqrt(jnp.float32(W))
    ex_norm = jnp.sqrt(lax.optimization_barrier(jnp.sum(example_sketch * example_sketch, axis=0)) + EPS)
    cand_norm = jnp.sqrt(lax.optimization_barrier(jnp.sum(candidate_sketch * candidate_sketch, axis=0)) + EPS)
    factor = scale / ex_norm
    picked = jnp.take(candidate_sketch, chosen, axis=1)
    picked_norm = jnp.take(cand_norm, chosen, axis=0)
    columns = jnp.dot(example_sketch.T, picked, precision=lax.Precision.HIGHEST, preferred_element_type=jnp.float32)
    columns = columns * factor[:, None] / picked_norm[None, :]
    bests = []
    best = best_start
    for step in range(ROUNDS):
        best = jnp.maximum(best, columns[:, step])
        bests.append(best)
    stacked = jnp.stack(bests)
    blocks = jnp.transpose(candidate_sketch.reshape(W, CANDIDATES // C_DEV, C_DEV), (1, 0, 2))
    block_norms = cand_norm.reshape(CANDIDATES // C_DEV, C_DEV)

    def one_block(pair):
        sketch, norms = pair
        similar = jnp.dot(example_sketch.T, sketch, precision=lax.Precision.HIGHEST, preferred_element_type=jnp.float32)
        similar = similar * factor[:, None] / norms[None, :]
        rows = [lax.optimization_barrier(jnp.sum(jnp.maximum(similar - stacked[step][:, None], 0.0), axis=0)) for step in range(ROUNDS)]
        return jnp.stack(rows)
    result = lax.map(one_block, (blocks, block_norms))
    gains = jnp.transpose(result, (1, 0, 2)).reshape(ROUNDS, CANDIDATES) / EXAMPLES
    return (best, gains)
```

```python
import functools

import jax
import jax.numpy as jnp
from jax import lax
from jax.experimental import pallas as pl
from jax.experimental.pallas import tpu as pltpu
from jax.sharding import PartitionSpec as P

EPS = 1e-06
CORES = 2
LANES = 128
SUBLANES = 8
F32 = jnp.float32
BF16 = jnp.bfloat16


def bits_of(n):
    return n.bit_length() - 1


def whole(shape):
    return jax.ShapeDtypeStruct(shape, F32)


def split_hi_lo(value):
    hi = value.astype(BF16)
    return hi, (value - hi.astype(F32)).astype(BF16)


def halves_kernel(place_ref, chosen_ref, cand_ref, same_ref, cross_ref, piece_ref):
    depth, width = cand_ref.shape
    half = width // CORES
    core, col = place_ref[0], place_ref[1]
    mine = pl.multiple_of(core * half, LANES)
    other = pl.multiple_of((CORES - 1 - core) * half, LANES)
    same_ref[...] = cand_ref[:, pl.ds(mine, half)]
    cross_ref[...] = cand_ref[:, pl.ds(other, half)]
    lane = lax.broadcasted_iota(jnp.int32, (depth, width), 1) + col * width
    spot = lax.broadcasted_iota(jnp.int32, (depth, LANES), 1)
    found = jnp.zeros((depth, LANES), F32)
    for step in range(chosen_ref.shape[0]):
        picked = jnp.where(lane == chosen_ref[step], cand_ref[...], 0.0)
        found = jnp.where(spot == step, jnp.sum(picked, axis=1, keepdims=True), found)
    piece_ref[...] = jnp.zeros_like(piece_ref)
    piece_ref[:, :depth] = found.T[: piece_ref.shape[0]]


def split_halves(place, chosen, cand):
    depth, width = cand.shape
    smem = pl.BlockSpec(memory_space=pltpu.SMEM)
    vmem = pl.BlockSpec(memory_space=pltpu.VMEM)
    half = whole((depth, width // CORES))
    return pl.pallas_call(
        halves_kernel,
        out_shape=(half, half, whole((SUBLANES, LANES))),
        in_specs=[smem, smem, vmem],
        out_specs=(vmem, vmem, vmem),
        name="halves",
    )(place, chosen, cand)


def examples_kernel(layout, place_ref, *refs):
    cols, rows, spans, depth_last = layout
    n = len(spans) * CORES
    pieces, (first_ref, last_ref), (full_ref,) = refs[:n], refs[n : n + 2], refs[n + 2 :]
    width, both = full_ref.shape
    count = both // CORES
    col_depth, row_depth = width // cols, width // rows
    row, col = place_ref[0], place_ref[1]
    for side in range(CORES):
        for (offset, start, size), ref in zip(spans, pieces[side * len(spans) :]):
            at = pl.multiple_of((col ^ offset) * col_depth + start, SUBLANES)
            full_ref[pl.ds(at, size), pl.ds(side * count, count)] = ref[...]
    chunk = min(512, count)
    depth_first = width - depth_last
    for begin in range(0, both, chunk):
        lanes = pl.ds(begin, chunk)
        total = jnp.sum(full_ref[:, lanes] * full_ref[:, lanes], axis=0, keepdims=True)
        factor = jnp.sqrt(F32(width)) / jnp.sqrt(total + EPS)
        slots = []
        for slot in range(rows):
            at = pl.multiple_of((row ^ slot) * row_depth, SUBLANES)
            slots.append(full_ref[pl.ds(at, row_depth), lanes] * factor)
        scaled = jnp.concatenate(slots, axis=0).T
        for ref, lo_at, size in ((first_ref, 0, depth_first), (last_ref, depth_first, depth_last)):
            hi, lo = split_hi_lo(scaled[:, lo_at : lo_at + size])
            ref[pl.ds(begin, chunk), 0:size] = hi
            ref[pl.ds(begin, chunk), size : 2 * size] = hi
            ref[pl.ds(begin, chunk), 2 * size : 3 * size] = lo


def prepare_examples(place, pieces, spans, cols, rows):
    width, count = pieces[0].shape[0] * cols, pieces[0].shape[1]
    depth_last = width // rows * CORES
    both = count * CORES
    vmem = pl.BlockSpec(memory_space=pltpu.VMEM)
    return pl.pallas_call(
        functools.partial(examples_kernel, (cols, rows, spans, depth_last)),
        out_shape=(
            jax.ShapeDtypeStruct((both, 3 * (width - depth_last)), BF16),
            jax.ShapeDtypeStruct((both, 3 * depth_last), BF16),
        ),
        in_specs=[pl.BlockSpec(memory_space=pltpu.SMEM)] + [vmem] * len(pieces),
        out_specs=(vmem, vmem),
        scratch_shapes=[pltpu.VMEM((width, both), F32)],
        name="examples",
    )(place, *pieces)


def best_kernel(rounds, first_ref, last_ref, vec_ref, mine_ref, other_ref, bests_ref, out_ref, parts_ref):
    step = pl.program_id(0)
    rows, _, _ = vec_ref.shape
    depth = first_ref.shape[1] // 3 + last_ref.shape[1] // 3
    row_depth = depth // rows
    depth_last = last_ref.shape[1] // 3
    depth_first = depth - depth_last

    @pl.when(step == 0)
    def _():
        vector = jnp.concatenate([vec_ref[slot][:, :row_depth] for slot in range(rows)], axis=1)
        norm = jnp.sqrt(jnp.sum(vector * vector, axis=1, keepdims=True) + EPS)
        tall = jnp.concatenate([vector / norm] * (LANES // SUBLANES), axis=0).T
        wide = [jnp.broadcast_to(tall[:, r : r + 1], (depth, LANES)) for r in range(rounds)]
        hi, lo = split_hi_lo(jnp.concatenate(wide, axis=1))
        for at, begin, size in ((0, 0, depth_first), (3 * depth_first, depth_first, depth_last)):
            parts_ref[at : at + size] = hi[begin : begin + size]
            parts_ref[at + size : at + 2 * size] = lo[begin : begin + size]
            parts_ref[at + 2 * size : at + 3 * size] = hi[begin : begin + size]

    cut = first_ref.shape[1]
    columns = jnp.dot(first_ref[...], parts_ref[:cut], preferred_element_type=F32)
    columns += jnp.dot(last_ref[...], parts_ref[cut:], preferred_element_type=F32)
    start = jnp.where(step == 0, mine_ref[...], other_ref[...])
    best = jnp.broadcast_to(start, (LANES, start.shape[1])).T
    for r in range(rounds):
        best = jnp.maximum(best, columns[:, r * LANES : (r + 1) * LANES])
        bests_ref[r] = best

    @pl.when(step == 0)
    def _():
        out_ref[...] = best.T[0:1]


def compute_best(first, last, vectors, mine, other, rounds):
    both = first.shape[0]
    count = both // CORES
    fixed = lambda shape: pl.BlockSpec(shape, lambda i: (0,) * len(shape))
    return pl.pallas_call(
        functools.partial(best_kernel, rounds),
        grid=(CORES,),
        out_shape=(whole((rounds, both, LANES)), whole((1, count))),
        in_specs=[
            pl.BlockSpec((count, first.shape[1]), lambda i: (i, 0)),
            pl.BlockSpec((count, last.shape[1]), lambda i: (i, 0)),
            fixed(vectors.shape),
            fixed((1, count)),
            fixed((1, count)),
        ],
        out_specs=(pl.BlockSpec((rounds, count, LANES), lambda i: (0, i, 0)), fixed((1, count))),
        scratch_shapes=[pltpu.VMEM((first.shape[1] + last.shape[1], rounds * LANES), BF16)],
        name="best",
    )(first, last, vectors, mine, other)


def stack_parts(ref, at, depth, value):
    size = value.shape[0]
    hi, lo = split_hi_lo(value)
    ref[at : at + size] = hi
    ref[depth + at : depth + at + size] = lo
    ref[2 * depth + at : 2 * depth + at + size] = hi


def early_kernel(groups, ex_ref, *refs):
    n = sum(groups)
    blocks, (acc_ref, square_ref), (parts_ref,) = refs[:n], refs[n : n + 2], refs[n + 2 :]

    @pl.when(pl.program_id(0) == 0)
    def _():
        at, taken = 0, 0
        square = jnp.zeros(square_ref.shape, F32)
        for group in groups:
            value = blocks[taken][...]
            for ref in blocks[taken + 1 : taken + group]:
                value += ref[...]
            taken += group
            for row in range(0, value.shape[0], SUBLANES):
                square += value[row : row + SUBLANES] * value[row : row + SUBLANES]
            stack_parts(parts_ref, at, ex_ref.shape[1] // 3, value)
            at += value.shape[0]
        square_ref[...] = square

    acc_ref[...] = jnp.dot(ex_ref[...], parts_ref[...], preferred_element_type=F32)


def early_products(first, slots, tile):
    both, depth3 = first.shape
    groups = tuple(len(slot) for slot in slots)
    flat = [block for slot in slots for block in slot]
    half = flat[0].shape[1]
    return pl.pallas_call(
        functools.partial(early_kernel, groups),
        grid=(both // tile,),
        out_shape=(whole((both, half)), whole((SUBLANES, half))),
        in_specs=[pl.BlockSpec((tile, depth3), lambda i: (i, 0))]
        + [pl.BlockSpec(block.shape, lambda i: (0, 0)) for block in flat],
        out_specs=(
            pl.BlockSpec((tile, half), lambda i: (i, 0)),
            pl.BlockSpec((SUBLANES, half), lambda i: (0, 0)),
        ),
        scratch_shapes=[pltpu.VMEM((depth3, half), BF16)],
        name="early",
    )(first, *flat)


def late_kernel(groups, total, ex_ref, acc_ref, square_ref, bests_ref, *refs):
    n = sum(groups)
    blocks, (out_ref,), (parts_ref, scale_ref, sums_ref) = refs[:n], refs[n : n + 1], refs[n + 1 :]
    step = pl.program_id(0)
    rounds = bests_ref.shape[0]
    tile, half = acc_ref.shape

    @pl.when(step == 0)
    def _():
        at, taken = 0, 0
        square = square_ref[...]
        for group in groups:
            value = blocks[taken][...]
            for ref in blocks[taken + 1 : taken + group]:
                value += ref[...]
            taken += group
            for row in range(0, value.shape[0], SUBLANES):
                square += value[row : row + SUBLANES] * value[row : row + SUBLANES]
            stack_parts(parts_ref, at, ex_ref.shape[1] // 3, value)
            at += value.shape[0]
        norm = jnp.sqrt(jnp.sum(square, axis=0, keepdims=True) + EPS)
        scale_ref[...] = jnp.broadcast_to(1.0 / norm, scale_ref.shape)
        sums_ref[...] = jnp.zeros_like(sums_ref)

    similar = acc_ref[...] + jnp.dot(ex_ref[...], parts_ref[...], preferred_element_type=F32)
    similar = similar.reshape(tile // SUBLANES, SUBLANES, half) * scale_ref[...][None]
    for r in range(rounds):
        best = bests_ref[r].reshape(tile // SUBLANES, SUBLANES, LANES)
        for at in range(0, half, LANES):
            gain = jnp.maximum(similar[:, :, at : at + LANES] - best, 0.0)
            sums_ref[r, :, at : at + LANES] += jnp.sum(gain, axis=0)

    @pl.when(step == pl.num_programs(0) - 1)
    def _():
        for r in range(rounds):
            out_ref[r : r + 1] = jnp.sum(sums_ref[r], axis=0, keepdims=True) / total


def late_gains(last, acc, square, bests, slots, total, tile):
    both, half = acc.shape
    rounds = bests.shape[0]
    groups = tuple(len(slot) for slot in slots)
    flat = [block for slot in slots for block in slot]
    depth3 = last.shape[1]
    return pl.pallas_call(
        functools.partial(late_kernel, groups, total),
        grid=(both // tile,),
        out_shape=whole((rounds, half)),
        in_specs=[
            pl.BlockSpec((tile, depth3), lambda i: (i, 0)),
            pl.BlockSpec((tile, half), lambda i: (i, 0)),
            pl.BlockSpec((SUBLANES, half), lambda i: (0, 0)),
            pl.BlockSpec((rounds, tile, LANES), lambda i: (0, i, 0)),
        ]
        + [pl.BlockSpec(block.shape, lambda i: (0, 0)) for block in flat],
        out_specs=pl.BlockSpec((rounds, half), lambda i: (0, 0)),
        scratch_shapes=[
            pltpu.VMEM((depth3, half), BF16),
            pltpu.VMEM((SUBLANES, half), F32),
            pltpu.VMEM((rounds, SUBLANES, half), F32),
        ],
        name="late",
    )(last, acc, square, bests, *flat)


def swap(value, axis, size, offset):
    return lax.ppermute(value, axis, [(i, i ^ offset) for i in range(size)])


def along_z(value, targets, rows, offset, flip):
    pairs = [
        ((z ^ offset) * CORES + (core ^ flip), z * CORES + core) for z in targets for core in range(CORES)
    ]
    return lax.ppermute(value, "row", pairs)


def on_device(cols, rows, example_sketch, candidate_sketch, best_start, chosen):
    chips = rows // CORES
    rounds = chosen.shape[0]
    row, col = lax.axis_index("row"), lax.axis_index("col")
    core = row % CORES
    i32 = lambda *values: jnp.stack(values).astype(jnp.int32)

    same, cross, piece = split_halves(i32(core, col), chosen, candidate_sketch)

    halves = (same, cross)
    got = {0: [[same], [swap(cross, "row", rows, 1)]]}
    evens = [d for d in range(2, chips, 2)]
    for d in evens + [1]:
        got[d] = [[along_z(halves[j], range(chips), rows, d, j)] for j in range(CORES)]
    for d in range(3, chips, 2):
        far = [z for z in range(chips) if abs((z ^ 1) - (z ^ d)) < abs(z - (z ^ d))]
        near = [z for z in range(chips) if z not in far]
        got[d] = []
        for j in range(CORES):
            direct = along_z(halves[j], near, rows, d, j)
            relayed = along_z(got[d ^ 1][j][0], far, rows, 1, 0)
            got[d].append([direct, relayed])
    slots = [got[d][j] for d in range(chips) for j in range(CORES)]

    for bit in range(bits_of(cols)):
        piece = piece + swap(piece, "col", cols, 1 << bit)
    vectors = piece[None]
    for bit in range(bits_of(rows)):
        vectors = jnp.concatenate([vectors, swap(vectors, "row", rows, 1 << bit)], axis=0)

    depth = example_sketch.shape[0]
    inner = 1 << ((bits_of(cols) + 1) // 2)
    spans, pieces, whole_of = [(0, 0, depth)], [example_sketch], {}
    for m in range(1, cols):
        if m % inner == 0 or m < inner:
            whole_of[m] = swap(example_sketch, "col", cols, m)
            spans.append((m, 0, depth))
            pieces.append(whole_of[m])
    for m in range(1, cols):
        low, high = m % inner, m - m % inner
        if low and high:
            cut = depth // 2
            spans.append((m, 0, cut))
            pieces.append(swap(whole_of[low][:cut], "col", cols, high))
            spans.append((m, cut, depth - cut))
            pieces.append(swap(whole_of[high][cut:], "col", cols, low))
    pieces = pieces + [swap(p, "row", rows, 1) for p in pieces]
    first, last = prepare_examples(i32(row, col), pieces, tuple(spans), cols, rows)

    start = best_start[None]
    bests, best = compute_best(first, last, vectors, start, swap(start, "row", rows, 1), rounds)

    tile = min(256, first.shape[0])
    acc, square = early_products(first, slots[:-CORES], tile)
    total = example_sketch.shape[1] * rows
    gains = late_gains(last, acc, square, bests, slots[-CORES:], total, tile)

    bit = 0
    while bit < bits_of(chips):
        width = min(2, bits_of(chips) - bit)
        terms = [gains] + [
            along_z(gains, range(chips), rows, k << bit, 0) for k in range(1, 1 << width)
        ]
        while len(terms) > 1:
            terms = [terms[i] + terms[i + 1] for i in range(0, len(terms), 2)]
        gains = terms[0]
        bit += width
    other = swap(gains, "row", rows, 1)
    lower = jnp.where(core == 0, gains, other)
    upper = jnp.where(core == 0, other, gains)
    return best[0], jnp.concatenate([lower, upper], axis=1)


def solution(mesh):
    in_specs = (P("col", "row"), P("row", "col"), P("row"), P())
    out_specs = (P("row"), P(None, "col"))
    body = functools.partial(on_device, mesh.shape["col"], mesh.shape["row"])
    return jax.shard_map(
        body, mesh=mesh, in_specs=in_specs, out_specs=out_specs, check_vma=False
    )
```
